32 devices in a mesh: rep: 2 (over y), branch: 4 (over z), leaf: 4 (over x, core).
Axes of the slice: x: 2, y: 2, z: 4, core: 2. Of those that a mesh axis runs over, the one named last changes fastest.
Arguments:
- queries: bfloat16 [4096, 4096], P(('rep', 'branch', 'leaf')), parts along dimension 0, may hold values from -8 to 8
- leaf_kv: bfloat16 [4096, 1024], P(('rep', 'branch', 'leaf')), parts along dimension 0, may hold values from -6 to 6
- branch_kv: bfloat16 [8192, 1024], P(('rep', 'branch', 'leaf')), parts along dimension 0, may hold values from -6 to 6
- root_kv: bfloat16 [4096, 1024], P(('rep', 'branch', 'leaf')), parts along dimension 0, may hold values from -8 to 8
- branch_len: int32 [16], P('rep'), parts along dimension 0, may hold values from 1 to 512, 3072 in all
- leaf_len: int32 [32], P(('rep', 'branch', 'leaf')), parts along dimension 0, may hold values from 1 to 128, 1536 in all
- leaf_parent: int32 [32], P(('rep', 'branch', 'leaf')), parts along dimension 0, may hold values from 0 to 7, as said below
Outputs:
- attended: bfloat16 [4096, 4096], P(('rep', 'branch', 'leaf')), parts along dimension 0
The draws below stay inside these ranges and needn't reach their ends.
There are 2 independent parts, one for each index of `rep`. The reference program is written for one: setup_inputs(seed, part) draws one part's arguments, and reference() takes and returns one part's arrays. A program takes and returns all parts, laid end to end along the dimension named above; each array names one. Nothing has to cross between parts.
Inputs may be any that keep to these rules, and one draw needn't show every extreme that they name: `leaf_parent`: leaf i's parent is one of the 2 branches of trunk i // 4, numbered from (i // 4) * 2; every branch is the parent of at least one leaf.
All inputs are finite; a program needn't handle non-finite values. No bound on the sum of `leaf_len` on one device may be relied on, other than what follows from the above.
Results may differ from the reference program's by a relative error of at most 0.005.
Values may be sent and summed in bfloat16 or wider, within the bound.
No kernel may reach another device: no remote copies, remote signals or barrier semaphores. Data moves between devices by JAX's collectives and lax.ppermute only.
A program may use at most 64 MiB of HBM per device.

```python
import math
import jax
import jax.numpy as jnp
import numpy as np
from jax import lax

QH = 32
KVH = 4
DH = 128
BR_DEV = 2
LQ = 128
BL = 512
ROOT = 2048
TRUNK_LEAVES = 4
LEAVES = 16
BRANCHES = 8


def draw_queries(key, part):
    base_key = jax.random.fold_in(key, 101)
    values = jnp.clip(2.0 * jax.random.normal(base_key, (LEAVES * LQ, QH * DH), jnp.float32), -8.0, 8.0)
    return values.astype(jnp.bfloat16)


def draw_root_kv(key, part):
    base_key = jax.random.fold_in(key, 202)
    kv_width = KVH * DH
    values = jnp.clip(jax.random.normal(base_key, (ROOT, 2 * kv_width), jnp.float32), -6.0, 6.0)
    return values.astype(jnp.bfloat16)


def shuffle_one(trunk_key):
    return jax.random.permutation(trunk_key, TRUNK_LEAVES)


def draw_leaf_parent(key, part):
    trunks = LEAVES // TRUNK_LEAVES
    trunk_keys = jax.random.split(jax.random.fold_in(key, 303), trunks)
    orders = jax.vmap(shuffle_one)(trunk_keys).astype(jnp.int32)
    rank_of = jnp.argsort(orders, axis=1).astype(jnp.int32)
    spare_pick = jax.random.randint(jax.random.fold_in(key, 304), (trunks, TRUNK_LEAVES), 0, BR_DEV, dtype=jnp.int32)
    local_pick = jnp.where(rank_of < BR_DEV, rank_of, spare_pick)
    first_branch = jnp.arange(trunks, dtype=jnp.int32)[:, None] * BR_DEV
    return (first_branch + local_pick).reshape(LEAVES).astype(jnp.int32)


def level_of(key, extent, pieces, smallest, top_value):
    factor_of = 1.0
    for axis_at, blocks in pieces:
        draws = jax.random.uniform(jax.random.fold_in(jax.random.fold_in(key, 6), axis_at), (blocks,), jnp.float32, smallest / len(pieces), top_value / len(pieces))
        factor_of = factor_of * jnp.repeat(jnp.exp(draws), extent[axis_at] // blocks).reshape((-1,) + (1,) * (len(extent) - 1 - axis_at))
    return factor_of


def length_profile(amount, total, reach, lean):
    weights = [(1 << 20) // math.isqrt(rank ** lean) + 1 for rank in range(2, amount + 1)]
    surplus, given = total - reach - (amount - 1), [1] * (amount - 1)
    while surplus > 0:
        candidates = [i for i in range(amount - 1) if given[i] < reach]
        whole, remaining = sum([weights[i] for i in candidates]), surplus
        for i in candidates:
            addition = min(reach - given[i], max(1, remaining * weights[i] // whole), surplus)
            given[i] = given[i] + addition
            surplus = surplus - addition
    return np.array([reach] + given)


def uneven(stream_key, amount, total, most, skew):
    if amount == 2:
        one = jax.random.randint(stream_key, (), max(1, total - most), min(most, total - 1) + 1)
        return jnp.stack([one, total - one])
    lengths = jnp.asarray(length_profile(amount, total, most, skew), jnp.int32)
    couples = (amount - 1) // 2
    giver, sink = lengths[1:1 + 2 * couples:2], lengths[2:2 + 2 * couples:2]
    room = jnp.minimum(giver - 1, most - sink)
    shifted = jax.random.randint(jax.random.fold_in(stream_key, 1), (couples,), 0, 1 << 20) % (room + 1)
    lengths = lengths.at[1:1 + 2 * couples:2].set(giver - shifted).at[2:2 + 2 * couples:2].set(sink + shifted)
    return lengths[jax.random.permutation(jax.random.fold_in(stream_key, 2), amount)]


def noise(own_key, shape, deviation, most, shards=(), kind=jnp.bfloat16):
    factor_of = level_of(own_key, shape, shards, -0.22, 0.18) if shards else 1.0
    values = jax.random.normal(own_key, shape, jnp.float32) * deviation * factor_of
    return jnp.minimum(jnp.maximum(values, -most), most).astype(kind)


def setup_inputs(seed: int = 0, part: int = 0) -> dict:
    key_of = jax.random.split(jax.random.key(seed), 8)
    part_splits = jax.random.split(jax.random.fold_in(key_of[7], part), 8)
    queries = draw_queries(jax.random.fold_in(jax.random.fold_in(key_of[7], part), 71), part)
    leaf_kv = noise(part_splits[1], (LEAVES * LQ, 2 * KVH * DH), 1.0, 6.0, ((0, 16),))
    branch_kv = noise(part_splits[2], (BRANCHES * BL, 2 * KVH * DH), 1.0, 6.0, ((0, 16),))
    root_kv = draw_root_kv(jax.random.fold_in(jax.random.fold_in(key_of[7], part), 71), part)
    branch_len = uneven(part_splits[4], BRANCHES, 3 * BRANCHES * BL // 4, BL, 1).astype(jnp.int32)
    leaf_len = uneven(part_splits[5], LEAVES, 3 * LEAVES * LQ // 4, LQ, 1).astype(jnp.int32)
    leaf_parent = draw_leaf_parent(jax.random.fold_in(jax.random.fold_in(key_of[7], part), 71), part)
    return dict(queries=queries, leaf_kv=leaf_kv, branch_kv=branch_kv, root_kv=root_kv, branch_len=branch_len, leaf_len=leaf_len, leaf_parent=leaf_parent)


def split_heads(kv_rows, kv_heads, head_size):
    kv_width = kv_heads * head_size
    key_rows = kv_rows[:, :kv_width].reshape(kv_rows.shape[0], kv_heads, head_size)
    value_rows = kv_rows[:, kv_width:].reshape(kv_rows.shape[0], kv_heads, head_size)
    return key_rows.astype(jnp.float32), value_rows.astype(jnp.float32)


def reference(queries, leaf_kv, branch_kv, root_kv, branch_len, leaf_len, leaf_parent):
    groups = QH // KVH
    inv_root = DH ** -0.5
    key_total = ROOT + BL + LQ
    column = jnp.arange(key_total, dtype=jnp.int32)[None, :]
    row_ids = jnp.arange(LQ, dtype=jnp.int32)[:, None]

    def one_leaf(leaf_index):
        parent = leaf_parent[leaf_index]
        query_rows = lax.dynamic_slice_in_dim(queries, (leaf_index * LQ).astype(jnp.int32), LQ, 0)
        query_rows = query_rows.reshape(LQ, KVH, groups, DH).astype(jnp.float32)
        branch_rows = lax.dynamic_slice_in_dim(branch_kv, (parent * BL).astype(jnp.int32), BL, 0)
        leaf_rows = lax.dynamic_slice_in_dim(leaf_kv, (leaf_index * LQ).astype(jnp.int32), LQ, 0)
        key_rows, value_rows = split_heads(jnp.concatenate([root_kv, branch_rows, leaf_rows], 0), KVH, DH)
        in_root = column < ROOT
        in_branch = (column >= ROOT) & (column < ROOT + branch_len[parent])
        in_leaf = (column >= ROOT + BL) & (column - ROOT - BL <= row_ids)
        visible = in_root | in_branch | in_leaf
        scores = jnp.einsum("qkgd,tkd->qkgt", query_rows, key_rows) * inv_root
        scores = jnp.where(visible[:, None, None, :], scores, -jnp.inf)
        row_max = jnp.max(scores, axis=-1, keepdims=True)
        weights = jnp.exp(scores - row_max)
        denominator = jnp.sum(weights, axis=-1)
        rounded = lax.optimization_barrier(weights.astype(jnp.bfloat16)).astype(jnp.float32)
        numerator = jnp.einsum("qkgt,tkd->qkgd", rounded, value_rows)
        attended = numerator / denominator[..., None]
        live_rows = (row_ids < leaf_len[leaf_index]).reshape(LQ, 1, 1, 1)
        attended = jnp.where(live_rows, attended, jnp.zeros_like(attended))
        return attended.reshape(LQ, QH * DH).astype(jnp.bfloat16)

    stacked = lax.map(one_leaf, jnp.arange(LEAVES, dtype=jnp.int32))
    return stacked.reshape(LEAVES * LQ, QH * DH)
```

```python
import functools
import math

import jax
import jax.numpy as jnp
from jax import lax
from jax.experimental import pallas as pl
from jax.experimental.pallas import tpu as pltpu
from jax.sharding import PartitionSpec as P

QH = 32
KVH = 4
DH = 128
BR_DEV = 2
BL = 512

neg_large = -1e30
key_tile = 256


def attend_kernel(kinds, table, query_ref, *refs):
    out_ref = refs[-1]
    row_count = query_ref.shape[0]
    groups = query_ref.shape[1] // DH
    total_rows = row_count * groups
    factor = DH ** -0.5 * math.log2(math.e)
    query = jnp.concatenate([query_ref[:, g * DH:(g + 1) * DH] for g in range(groups)], axis=0)
    row_max = jnp.full((total_rows, 1), neg_large, jnp.float32)
    total = None
    for number, kind in enumerate(kinds):
        key_ref, value_ref = refs[2 * number], refs[2 * number + 1]
        key_count = key_ref.shape[0]
        for start in range(0, key_count, key_tile):
            size = min(key_tile, key_count - start)
            keys = key_ref[start:start + size, :]
            values = value_ref[start:start + size, :]
            scores = lax.dot_general(
                query, keys, (((1,), (1,)), ((), ())), preferred_element_type=jnp.float32
            )
            if kind != "root":
                column = lax.broadcasted_iota(jnp.int32, scores.shape, 1) + start
                if kind == "leaf":
                    row = lax.rem(lax.broadcasted_iota(jnp.int32, scores.shape, 0), row_count)
                    visible = column <= row
                else:
                    visible = column < table[1]
                scores = jnp.where(visible, scores, neg_large)
            new_max = jnp.maximum(row_max, jnp.max(scores, axis=1, keepdims=True))
            weights = jnp.exp2((scores - new_max) * factor).astype(jnp.bfloat16)
            padded = jnp.concatenate([values, jnp.ones_like(values)], axis=1)
            product = jnp.dot(weights, padded, preferred_element_type=jnp.float32)
            if total is None:
                total = product
            else:
                total = total * jnp.exp2((row_max - new_max) * factor) + product
            row_max = new_max
    result = total[:, :DH] / total[:, DH:]
    live = lax.broadcasted_iota(jnp.int32, (row_count, DH), 0) < table[2]
    for g in range(groups):
        piece = result[g * row_count:(g + 1) * row_count]
        out_ref[:, g * DH:(g + 1) * DH] = jnp.where(live, piece, 0.0).astype(out_ref.dtype)


def attend(table, queries, leaf_rows, trunk_rows, root_rows):
    row_count = queries.shape[0]
    groups = QH // KVH
    query_spec = pl.BlockSpec((row_count, groups * DH), lambda k, t: (0, k))
    in_specs = [query_spec]
    operands = [queries]
    kinds = []
    for kind, rows, block in (("leaf", leaf_rows, None), ("branch", trunk_rows, BL), ("root", root_rows, None)):
        height = rows.shape[0] if block is None else block
        for offset in (0, KVH):
            if kind == "branch":
                spec = pl.BlockSpec((height, DH), lambda k, t, offset=offset: (t[0], k + offset))
            else:
                spec = pl.BlockSpec((height, DH), lambda k, t, offset=offset: (0, k + offset))
            in_specs.append(spec)
            operands.append(rows)
        kinds.append(kind)
    return pl.pallas_call(
        functools.partial(attend_kernel, tuple(kinds)),
        grid_spec=pltpu.PrefetchScalarGridSpec(
            num_scalar_prefetch=1, grid=(KVH,), in_specs=in_specs, out_specs=query_spec
        ),
        out_shape=jax.ShapeDtypeStruct(queries.shape, queries.dtype),
        compiler_params=pltpu.CompilerParams(vmem_limit_bytes=60 * 1024 * 1024),
        name="attend",
    )(table, *operands)


def body(queries, leaf_kv, branch_kv, root_kv, branch_len, leaf_len, leaf_parent):
    trunk_rows = lax.all_gather(branch_kv, "leaf", axis=0, tiled=True)
    whole_root = lax.all_gather(root_kv, ("branch", "leaf"), axis=0, tiled=True)
    parent = leaf_parent[0]
    local_branch = parent - lax.axis_index("branch") * BR_DEV
    table = jnp.stack([local_branch, branch_len[parent], leaf_len[0]])
    return attend(table, queries, leaf_kv, trunk_rows, whole_root)


def solution(mesh):
    split = P(("rep", "branch", "leaf"), None)
    single = P(("rep", "branch", "leaf"))
    return jax.shard_map(
        body,
        mesh=mesh,
        in_specs=(split, split, split, split, P("rep"), single, single),
        out_specs=split,
        check_vma=False,
    )
```

```python
import functools
import math

import jax
import jax.numpy as jnp
from jax import lax
from jax.experimental import pallas as pl
from jax.experimental.pallas import tpu as pltpu
from jax.sharding import PartitionSpec as P


QH = 32
KVH = 4
DH = 128
BR_DEV = 2
BL = 512


neg_large = -1e30
key_tile = 256
kernel_vmem = 24 * 1024 * 1024


def load_tile(pieces, refs, start, size):
    parts = []
    first = 0
    for number, height in pieces:
        low, high = max(start, first), min(start + size, first + height)
        if low < high:
            parts.append(refs[number][low - first:high - first, :])
        first += height
    return parts[0] if len(parts) == 1 else jnp.concatenate(parts, axis=0)


def attend_kernel(spans, carries, finishes, table, query_ref, *refs):
    row_count = query_ref.shape[0]
    groups = query_ref.shape[1] // DH
    total_rows = row_count * groups
    factor = DH ** -0.5 * math.log2(math.e)
    operand_count = 2 * sum(len(pieces) for kind, pieces in spans)
    key_refs = refs[:operand_count:2]
    value_refs = refs[1:operand_count:2]
    rest = refs[operand_count:]
    query = jnp.concatenate([query_ref[:, g * DH:(g + 1) * DH] for g in range(groups)], axis=0)
    if carries:
        total = jnp.concatenate([rest[0][...], jnp.ones((total_rows, DH), jnp.float32)], axis=1)
        row_max = jnp.max(rest[1][...], axis=1, keepdims=True)
        rest = rest[2:]
    else:
        row_max = jnp.full((total_rows, 1), neg_large, jnp.float32)
        total = None
    for kind, pieces in spans:
        key_count = sum(height for number, height in pieces)
        for start in range(0, key_count, key_tile):
            size = min(key_tile, key_count - start)
            keys = load_tile(pieces, key_refs, start, size)
            values = load_tile(pieces, value_refs, start, size)
            scores = lax.dot_general(
                query, keys, (((1,), (1,)), ((), ())), preferred_element_type=jnp.float32
            )
            if kind != "root":
                column = lax.broadcasted_iota(jnp.int32, scores.shape, 1) + start
                if kind == "leaf":
                    row = lax.rem(lax.broadcasted_iota(jnp.int32, scores.shape, 0), row_count)
                    visible = column <= row
                else:
                    visible = column < table[1]
                scores = jnp.where(visible, scores, neg_large)
            new_max = jnp.maximum(row_max, jnp.max(scores, axis=1, keepdims=True))
            weights = jnp.exp2((scores - new_max) * factor).astype(jnp.bfloat16)
            padded = jnp.concatenate([values, jnp.ones_like(values)], axis=1)
            product = jnp.dot(weights, padded, preferred_element_type=jnp.float32)
            if total is None:
                total = product
            else:
                total = total * jnp.exp2((row_max - new_max) * factor) + product
            row_max = new_max
    result = total[:, :DH] / total[:, DH:]
    if finishes:
        out_ref = rest[0]
        live = lax.broadcasted_iota(jnp.int32, (row_count, DH), 0) < table[2]
        for g in range(groups):
            piece = result[g * row_count:(g + 1) * row_count]
            out_ref[:, g * DH:(g + 1) * DH] = jnp.where(live, piece, 0.0).astype(out_ref.dtype)
    else:
        rest[0][...] = result
        rest[1][...] = row_max + jnp.log2(total[:, DH:]) * (1.0 / factor)


def attend(table, queries, spans, state=None, finishes=False):
    row_count = queries.shape[0]
    groups = QH // KVH
    query_spec = pl.BlockSpec((row_count, groups * DH), lambda k, t: (0, k))
    state_spec = pl.BlockSpec((row_count * groups, DH), lambda k, t: (k, 0))
    in_specs, operands, described = [query_spec], [queries], []
    number = 0
    key_count = 0
    for kind, pieces in spans:
        listed = []
        for rows, block in pieces:
            height = rows.shape[0] if block is None else block
            for offset in (0, KVH):
                if block is None:
                    index = lambda k, t, offset=offset: (0, k + offset)
                else:
                    index = lambda k, t, offset=offset: (t[0], k + offset)
                in_specs.append(pl.BlockSpec((height, DH), index))
                operands.append(rows)
            listed.append((number, height))
            number += 1
            key_count += height
        described.append((kind, tuple(listed)))
    if state is not None:
        in_specs.extend((state_spec, state_spec))
        operands.extend(state)
    if finishes:
        out_specs = query_spec
        out_shape = jax.ShapeDtypeStruct(queries.shape, queries.dtype)
    else:
        out_specs = (state_spec, state_spec)
        part = jax.ShapeDtypeStruct((KVH * row_count * groups, DH), jnp.float32)
        out_shape = (part, part)
    return pl.pallas_call(
        functools.partial(attend_kernel, tuple(described), state is not None, finishes),
        grid_spec=pltpu.PrefetchScalarGridSpec(
            num_scalar_prefetch=1, grid=(KVH,), in_specs=in_specs, out_specs=out_specs
        ),
        out_shape=out_shape,
        compiler_params=pltpu.CompilerParams(vmem_limit_bytes=kernel_vmem),
        cost_estimate=pl.CostEstimate(
            flops=4 * row_count * QH * DH * key_count,
            bytes_accessed=2 * row_count * QH * DH * 4,
            transcendentals=row_count * QH * key_count,
        ),
    )(table, *operands)


def gathered_body(queries, leaf_kv, branch_kv, root_kv, branch_len, leaf_len, leaf_parent):
    trunk_rows = lax.all_gather(branch_kv, "leaf", axis=0, tiled=True)
    whole_root = lax.all_gather(root_kv, ("branch", "leaf"), axis=0, tiled=True)
    parent = leaf_parent[0]
    local_branch = parent - lax.axis_index("branch") * BR_DEV
    table = jnp.stack([local_branch, branch_len[parent], leaf_len[0]])
    spans = [("leaf", [(leaf_kv, None)]), ("branch", [(trunk_rows, BL)]), ("root", [(whole_root, None)])]
    return attend(table, queries, spans, finishes=True)


def exchanged_body(queries, leaf_kv, branch_kv, root_kv, branch_len, leaf_len, leaf_parent):
    across = [(i, i ^ 2) for i in range(4)]
    beside = [(i, i ^ 1) for i in range(4)]
    near = [(i, i ^ 1) for i in range(4)]
    far = [(i, i ^ 3) for i in range(4)]
    cross = [(1, 0), (2, 3), (3, 1), (0, 2)]

    def swap(rows):
        return lax.ppermute(rows, "leaf", beside)

    z = lax.axis_index("branch")
    at_end = (z == 0) | (z == 3)
    parent = leaf_parent[0]
    local_branch = parent - z * BR_DEV
    place = lax.axis_index("leaf")
    elsewhere = local_branch != place // 2
    table = jnp.stack([jnp.int32(0), branch_len[parent], leaf_len[0]])

    own = root_kv
    far_own = lax.ppermute(own, "branch", far)
    near_own = lax.ppermute(own, "branch", near)
    side = lax.ppermute(own, "leaf", across)
    branch_side = lax.ppermute(branch_kv, "leaf", across)
    own_swapped = swap(own)
    branch_swapped = swap(branch_kv)
    state = attend(table, queries, [("leaf", [(leaf_kv, None)]), ("root", [(own, None), (own_swapped, None)])])

    cross_own = lax.ppermute(jnp.where(at_end, own, far_own), "branch", cross)
    near_side = lax.ppermute(side, "branch", near)
    far_side = lax.ppermute(far_own, "leaf", across)
    side_swapped = swap(side)
    near_own_swapped = swap(near_own)
    far_own_swapped = swap(far_own)
    branch_side_swapped = swap(branch_side)
    held = jnp.where(elsewhere, branch_side, branch_kv)
    swapped = jnp.where(elsewhere, branch_side_swapped, branch_swapped)
    first = place % 2 == 0
    low = jnp.where(first, held, swapped)
    high = jnp.where(first, swapped, held)
    state = attend(table, queries, [
        ("root", [(rows, None) for rows in (
            side, side_swapped, near_own, near_own_swapped, far_own, far_own_swapped)]),
        ("branch", [(low, None), (high, None)]),
    ], state)

    cross_side = lax.ppermute(jnp.where(at_end, side, far_side), "branch", cross)
    near_side_swapped = swap(near_side)
    far_side_swapped = swap(far_side)
    cross_own_swapped = swap(cross_own)
    state = attend(table, queries, [
        ("root", [(rows, None) for rows in (
            near_side, near_side_swapped, far_side, far_side_swapped, cross_own, cross_own_swapped)]),
    ], state)
    cross_side_swapped = swap(cross_side)
    return attend(table, queries, [("root", [(cross_side, None), (cross_side_swapped, None)])], state, finishes=True)


def solution(mesh):
    split = P(("rep", "branch", "leaf"), None)
    single = P(("rep", "branch", "leaf"))
    small = mesh.shape["branch"] == 4 and mesh.shape["leaf"] == 4
    return jax.shard_map(
        exchanged_body if small else gathered_body,
        mesh=mesh,
        in_specs=(split, split, split, split, P("rep"), single, single),
        out_specs=split,
        check_vma=False,
    )
```

```python
import functools
import math

import jax
import jax.numpy as jnp
from jax import lax
from jax.experimental import pallas as pl
from jax.experimental.pallas import tpu as pltpu
from jax.sharding import PartitionSpec as P


QH = 32
KVH = 4
DH = 128
BR_DEV = 2
BL = 512


neg_large = -1e30
key_tile = 256
kernel_vmem = 28 * 1024 * 1024
vmem = pl.BlockSpec(memory_space=pltpu.VMEM)
smem = pl.BlockSpec(memory_space=pltpu.SMEM)
anywhere = pl.BlockSpec(memory_space=pl.ANY)


def tiles_of(spans, scalars):
    tiles = []
    for kind, refs in spans:
        if kind == "root":
            pending, height = [], 0
            for ref in refs:
                for start in range(0, ref.shape[0], key_tile):
                    size = min(key_tile, ref.shape[0] - start)
                    pending.append((ref, start, size))
                    height += size
                    if height >= key_tile:
                        tiles.append((pending, height, None, None))
                        pending, height = [], 0
            if pending:
                tiles.append((pending, height, None, None))
        elif kind == "leaf":
            tiles.append(([(refs[0], 0, refs[0].shape[0])], refs[0].shape[0], "leaf", 0))
        elif kind == "trunk":
            base = scalars["local_branch"] * BL
            for start in range(0, BL, key_tile):
                tiles.append(([(refs[0], base + start, key_tile)], key_tile, "branch", start))
        else:
            half = refs[0].shape[0]
            first = scalars["core"] * half
            tiles.append(([refs[0:2]], half, "branch", first))
            tiles.append(([refs[2:4]], half, "branch", half - first))
    return tiles


def load(parts, lanes, scalars):
    pieces = []
    for part in parts:
        if len(part) == 2:
            near, far = part
            pieces.append(jnp.where(scalars["elsewhere"], far[:, lanes], near[:, lanes]))
        else:
            ref, start, size = part
            if not isinstance(start, int):
                start = pl.multiple_of(start, key_tile)
            pieces.append(ref[pl.ds(start, size), lanes])
    return pieces[0] if len(pieces) == 1 else jnp.concatenate(pieces, axis=0)


def attend_kernel(kinds, carries, finishes, *refs):
    refs = list(refs)
    scalars = {}
    if any(kind in ("trunk", "branch") for kind, count in kinds):
        parent_ref, length_ref = refs.pop(0), refs.pop(0)
        parent = parent_ref[0]
        place = lax.axis_index("leaf")
        local_branch = parent - lax.axis_index("branch") * BR_DEV
        scalars = dict(
            local_branch=local_branch,
            length=length_ref[parent],
            core=lax.rem(place, 2),
            elsewhere=local_branch != lax.div(place, 2),
        )
    live_ref = refs.pop(0) if finishes else None
    query_ref = refs.pop(0)
    spans = [(kind, [refs.pop(0) for _ in range(count)]) for kind, count in kinds]
    if carries:
        old_total, old_max = refs.pop(0), refs.pop(0)
    tiles = tiles_of(spans, scalars)
    row_count = query_ref.shape[0]
    groups = query_ref.shape[1] // (DH * KVH)
    total_rows = row_count * groups
    factor = DH ** -0.5 * math.log2(math.e)

    def head(k, unused):
        def lanes_at(number):
            return pl.ds(pl.multiple_of(number * DH, DH), DH)

        rows = pl.ds(pl.multiple_of(k * total_rows, total_rows), total_rows)
        query = jnp.concatenate([query_ref[:, lanes_at(k * groups + g)] for g in range(groups)], axis=0)
        if carries:
            total = jnp.concatenate([old_total[rows, :], jnp.ones((total_rows, DH), jnp.float32)], axis=1)
            row_max = jnp.max(old_max[rows, :], axis=1, keepdims=True)
        else:
            row_max = jnp.full((total_rows, 1), neg_large, jnp.float32)
            total = None
        for parts, size, mask, offset in tiles:
            keys = load(parts, lanes_at(k), scalars)
            values = load(parts, lanes_at(KVH + k), scalars)
            scores = lax.dot_general(
                query, keys, (((1,), (1,)), ((), ())), preferred_element_type=jnp.float32
            )
            if mask is not None:
                column = lax.broadcasted_iota(jnp.int32, scores.shape, 1)
                if mask == "leaf":
                    row = lax.rem(lax.broadcasted_iota(jnp.int32, scores.shape, 0), row_count)
                    visible = column <= row
                else:
                    visible = column < scalars["length"] - offset
                scores = jnp.where(visible, scores, neg_large)
            new_max = jnp.maximum(row_max, jnp.max(scores, axis=1, keepdims=True))
            weights = jnp.exp2((scores - new_max) * factor).astype(jnp.bfloat16)
            padded = jnp.concatenate([values, jnp.ones_like(values)], axis=1)
            product = jnp.dot(weights, padded, preferred_element_type=jnp.float32)
            if total is None:
                total = product
            else:
                total = total * jnp.exp2((row_max - new_max) * factor) + product
            row_max = new_max
        result = total[:, :DH] / total[:, DH:]
        if finishes:
            out_ref, held_ref, sems = refs
            live = lax.broadcasted_iota(jnp.int32, (row_count, DH), 0) < live_ref[0]
            for g in range(groups):
                piece = result[g * row_count:(g + 1) * row_count]
                held_ref[k, :, g * DH:(g + 1) * DH] = jnp.where(live, piece, 0.0).astype(held_ref.dtype)
            pltpu.make_async_copy(held_ref.at[k], out_of(out_ref, k), sems.at[k]).start()
        else:
            refs[0][rows, :] = result
            refs[1][rows, :] = row_max + jnp.log2(total[:, DH:]) * (1.0 / factor)
        return unused

    def out_of(out_ref, k):
        width = groups * DH
        return out_ref.at[:, pl.ds(pl.multiple_of(k * width, width), width)]

    lax.fori_loop(0, KVH, head, 0)
    if finishes:
        out_ref, held_ref, sems = refs
        for k in range(KVH):
            pltpu.make_async_copy(held_ref.at[k], out_of(out_ref, k), sems.at[k]).wait()


def attend(numbers, queries, spans, state=None, finishes=False):
    row_count = queries.shape[0]
    groups = QH // KVH
    parent, branch_len, leaf_len = numbers
    operands, in_specs = [], []
    if any(kind in ("trunk", "branch") for kind, arrays in spans):
        operands += [parent, branch_len]
        in_specs += [smem, smem]
    if finishes:
        operands.append(leaf_len)
        in_specs.append(smem)
    arrays = [queries] + [array for kind, listed in spans for array in listed]
    operands += arrays
    in_specs += [vmem] * len(arrays)
    aliases = {}
    if state is not None:
        if not finishes:
            aliases = {len(operands): 0, len(operands) + 1: 1}
        operands += state
        in_specs += [vmem, vmem]
    scratch = ()
    if finishes:
        out_specs = anywhere
        out_shape = jax.ShapeDtypeStruct(queries.shape, queries.dtype)
        scratch = (
            pltpu.VMEM((KVH, row_count, groups * DH), queries.dtype),
            pltpu.SemaphoreType.DMA((KVH,)),
        )
    else:
        part = jax.ShapeDtypeStruct((KVH * row_count * groups, DH), jnp.float32)
        out_specs, out_shape = [vmem, vmem], [part, part]
    key_count = sum(array.shape[0] for kind, listed in spans for array in listed)
    return pl.pallas_call(
        functools.partial(
            attend_kernel, tuple((kind, len(listed)) for kind, listed in spans), state is not None, finishes
        ),
        in_specs=in_specs,
        out_specs=out_specs,
        out_shape=out_shape,
        scratch_shapes=scratch,
        input_output_aliases=aliases,
        compiler_params=pltpu.CompilerParams(vmem_limit_bytes=kernel_vmem),
        cost_estimate=pl.CostEstimate(
            flops=4 * row_count * QH * DH * key_count,
            bytes_accessed=2 * row_count * QH * DH * 4,
            transcendentals=row_count * QH * key_count,
        ),
    )(*operands)


def pick_kernel(end_ref, middle_ref, out_ref):
    z = lax.axis_index("branch")
    at_end = (z == 0) | (z == lax.axis_size("branch") - 1)

    @pl.when(at_end)
    def _():
        out_ref[...] = end_ref[...]

    @pl.when(jnp.logical_not(at_end))
    def _():
        out_ref[...] = middle_ref[...]


def pick(end_rows, middle_rows):
    return pl.pallas_call(
        pick_kernel,
        in_specs=[vmem, vmem],
        out_specs=vmem,
        out_shape=jax.ShapeDtypeStruct(end_rows.shape, end_rows.dtype),
        compiler_params=pltpu.CompilerParams(vmem_limit_bytes=4 * 1024 * 1024),
    )(end_rows, middle_rows)


def gathered_body(queries, leaf_kv, branch_kv, root_kv, branch_len, leaf_len, leaf_parent):
    trunk_rows = lax.all_gather(branch_kv, "leaf", axis=0, tiled=True)
    whole_root = lax.all_gather(root_kv, ("branch", "leaf"), axis=0, tiled=True)
    numbers = (leaf_parent, branch_len, leaf_len)
    spans = [("leaf", [leaf_kv]), ("trunk", [trunk_rows]), ("root", [whole_root])]
    return attend(numbers, queries, spans, finishes=True)


def exchanged_body(queries, leaf_kv, branch_kv, root_kv, branch_len, leaf_len, leaf_parent):
    across = [(i, i ^ 2) for i in range(4)]
    beside = [(i, i ^ 1) for i in range(4)]
    near = [(i, i ^ 1) for i in range(4)]
    far = [(i, i ^ 3) for i in range(4)]
    cross = [(1, 0), (2, 3), (3, 1), (0, 2)]
    numbers = (leaf_parent, branch_len, leaf_len)

    def swap(rows):
        return lax.ppermute(rows, "leaf", beside)

    own = root_kv
    far_own = lax.ppermute(own, "branch", far)
    near_own = lax.ppermute(own, "branch", near)
    side = lax.ppermute(own, "leaf", across)
    branch_side = lax.ppermute(branch_kv, "leaf", across)
    own_swapped = swap(own)
    branch_swapped = swap(branch_kv)
    state = attend(numbers, queries, [("leaf", [leaf_kv]), ("root", [own, own_swapped])])

    cross_own = lax.ppermute(pick(own, far_own), "branch", cross)
    near_side = lax.ppermute(side, "branch", near)
    far_side = lax.ppermute(far_own, "leaf", across)
    side_swapped = swap(side)
    near_own_swapped = swap(near_own)
    far_own_swapped = swap(far_own)
    branch_side_swapped = swap(branch_side)
    state = attend(numbers, queries, [
        ("root", [side, near_own, far_own, side_swapped, near_own_swapped, far_own_swapped]),
    ], state)

    cross_side = lax.ppermute(pick(side, far_side), "branch", cross)
    near_side_swapped = swap(near_side)
    far_side_swapped = swap(far_side)
    cross_own_swapped = swap(cross_own)
    state = attend(numbers, queries, [("branch", [branch_kv, branch_side, branch_swapped, branch_side_swapped])], state)
    state = attend(numbers, queries, [
        ("root", [near_side, far_side, cross_own, near_side_swapped, far_side_swapped, cross_own_swapped]),
    ], state)
    cross_side_swapped = swap(cross_side)
    return attend(numbers, queries, [("root", [cross_side, cross_side_swapped])], state, finishes=True)


def solution(mesh):
    split = P(("rep", "branch", "leaf"), None)
    single = P(("rep", "branch", "leaf"))
    small = mesh.shape["branch"] == 4 and mesh.shape["leaf"] == 4
    return jax.shard_map(
        exchanged_body if small else gathered_body,
        mesh=mesh,
        in_specs=(split, split, split, split, P("rep"), single, single),
        out_specs=split,
        check_vma=False,
    )
```

```python
import functools
import math

import jax
import jax.numpy as jnp
from jax import lax
from jax.experimental import pallas as pl
from jax.experimental.pallas import tpu as pltpu
from jax.sharding import PartitionSpec as P


QH = 32
KVH = 4
DH = 128
BR_DEV = 2
BL = 512


neg_large = -1e30
key_tile = 256
head_block = 4
group_block = 8
kernel_vmem = 28 * 1024 * 1024
vmem = pl.BlockSpec(memory_space=pltpu.VMEM)
smem = pl.BlockSpec(memory_space=pltpu.SMEM)
anywhere = pl.BlockSpec(memory_space=pl.ANY)
hbm = pl.BlockSpec(memory_space=pltpu.HBM)


def tiles_of(spans, scalars):
    tiles, pending, height = [], [], 0
    for kind, refs in spans:
        parts = []
        if kind == "leaf":
            tiles.append(([((refs[0], refs[0]), 0, refs[0].shape[0], None)], True))
        elif kind == "root":
            for ref in refs:
                for start in range(0, ref.shape[0], key_tile):
                    parts.append(((ref, ref), start, min(key_tile, ref.shape[0] - start), None))
        elif kind == "trunk":
            base = scalars["local_branch"] * BL
            for start in range(0, BL, key_tile):
                parts.append(((refs[0], refs[0]), base + start, key_tile, start))
        else:
            rows = refs[0].shape[0]
            place = scalars["core"] if kind[0] == "held" else 1 - scalars["core"]
            parts.append((tuple(refs), 0, rows, (place * 2 + kind[1]) * rows))
        for part in parts:
            pending.append(part)
            height += part[2]
            if height >= key_tile:
                tiles.append((pending, False))
                pending, height = [], 0
    if pending:
        tiles.append((pending, False))
    return tiles


def load(part, lanes, scalars):
    (near, far), start, size, token = part
    if not isinstance(start, int):
        start = pl.multiple_of(start, key_tile)
    rows = near[pl.ds(start, size), lanes]
    if far is not near:
        rows = jnp.where(scalars["elsewhere"], far[pl.ds(start, size), lanes], rows)
    return rows


def joined(parts):
    return parts[0] if len(parts) == 1 else jnp.concatenate(parts, axis=0)


def attend_kernel(kinds, form, *refs):
    refs = list(refs)
    reads_numbers, finishes = form in ("first", "only"), form in ("last", "only")
    masks = any(kind not in ("leaf", "root") for kind, count in kinds)
    if reads_numbers:
        parent_ref, length_ref, live_ref = [refs.pop(0) for _ in range(3)]
        parent = parent_ref[0]
        local_branch = parent - lax.axis_index("branch") * BR_DEV
        length, live_count = length_ref[parent], live_ref[0]
    elif masks or finishes:
        info = refs.pop(0)[...]
        local_branch, length, live_count = [jnp.max(info[number:number + 1]) for number in range(3)]
    query_ref = refs.pop(0)
    spans = [(kind, [refs.pop(0) for _ in range(count)]) for kind, count in kinds]
    carries = not reads_numbers
    if carries:
        old_total, old_max = refs.pop(0), refs.pop(0)
    if finishes:
        out_ref, held_ref, sems = refs
    else:
        total_ref, max_ref = refs.pop(0), refs.pop(0)
    if form == "first":
        info_ref = refs.pop(0)
        row = lax.broadcasted_iota(jnp.int32, info_ref.shape, 0)
        info_ref[...] = jnp.where(row == 0, local_branch, jnp.where(row == 1, length, live_count))
    scalars = {}
    if masks:
        place = lax.axis_index("leaf")
        scalars = dict(
            local_branch=local_branch,
            length=length,
            core=lax.rem(place, 2),
            elsewhere=local_branch != lax.div(place, 2),
        )
        seen_ref = [listed for kind, listed in spans if kind == "root"][0][0]
    tiles = tiles_of(spans, scalars)
    row_count = query_ref.shape[0]
    groups = query_ref.shape[1] // (DH * KVH)
    factor = DH ** -0.5 * math.log2(math.e)

    def lanes_at(number):
        start = number * DH
        return pl.ds(start if isinstance(start, int) else pl.multiple_of(start, DH), DH)

    def head(k, g0):
        total_rows = row_count * group_block
        start = (k * groups + g0) * row_count
        rows = pl.ds(start if isinstance(start, int) else pl.multiple_of(start, row_count), total_rows)
        query = jnp.concatenate(
            [query_ref[:, lanes_at(k * groups + g)] for g in range(g0, g0 + group_block)], axis=0
        )
        if carries:
            total = old_total[rows, :]
            row_max = old_max[rows, :]
        else:
            row_max, total = None, None
        for parts, causal in tiles:
            keys, values, ones = [], [], []
            for part in parts:
                key_rows = load(part, lanes_at(k), scalars)
                value_rows = load(part, lanes_at(KVH + k), scalars)
                one_rows = jnp.ones_like(value_rows)
                if part[3] is not None:
                    used = lax.broadcasted_iota(jnp.int32, key_rows.shape, 0) < scalars["length"] - part[3]
                    seen = seen_ref[:16, lanes_at(k)][:1].astype(jnp.float32)
                    key_rows = jnp.where(used, key_rows.astype(jnp.float32), seen).astype(key_rows.dtype)
                    value_rows = jnp.where(used, value_rows.astype(jnp.float32), 0.0).astype(key_rows.dtype)
                    one_rows = jnp.where(used, 1.0, 0.0).astype(key_rows.dtype)
                keys.append(key_rows)
                values.append(value_rows)
                ones.append(one_rows)
            scores = lax.dot_general(
                query, joined(keys), (((1,), (1,)), ((), ())), preferred_element_type=jnp.float32
            )
            if causal:
                column = lax.broadcasted_iota(jnp.int32, scores.shape, 1)
                row = lax.rem(lax.broadcasted_iota(jnp.int32, scores.shape, 0), row_count)
                scores = jnp.where(column <= row, scores, neg_large)
            top = jnp.broadcast_to(jnp.max(scores, axis=1, keepdims=True), (total_rows, DH))
            new_max = top if row_max is None else jnp.maximum(row_max, top)
            wide = jnp.concatenate([new_max] * (scores.shape[1] // DH), axis=1)
            weights = jnp.exp2((scores - wide) * factor).astype(jnp.bfloat16)
            padded = jnp.concatenate([joined(values), joined(ones)], axis=1)
            product = jnp.dot(weights, padded, preferred_element_type=jnp.float32)
            if total is None:
                total = product
            else:
                shrink = jnp.exp2((row_max - new_max) * factor)
                total = total * jnp.concatenate([shrink, shrink], axis=1) + product
            row_max = new_max
        if finishes:
            result = total[:, :DH] * pl.reciprocal(total[:, DH:])
            live = lax.broadcasted_iota(jnp.int32, (row_count, DH), 0) < live_count
            for g in range(group_block):
                piece = result[g * row_count:(g + 1) * row_count]
                lanes = slice((g0 + g) * DH, (g0 + g + 1) * DH)
                held_ref[k, :, lanes] = jnp.where(live, piece, 0.0).astype(held_ref.dtype)
            if g0 + group_block == groups:
                pltpu.make_async_copy(held_ref.at[k], out_of(out_ref, k), sems.at[k]).start()
        else:
            total_ref[rows, :] = total
            max_ref[rows, :] = row_max

    def out_of(out_ref, k):
        width = groups * DH
        start = k * width
        return out_ref.at[:, pl.ds(start if isinstance(start, int) else pl.multiple_of(start, width), width)]

    def heads(step, unused):
        for extra in range(head_block):
            for g0 in range(0, groups, group_block):
                head(step * head_block + extra, g0)
        return unused

    if head_block == KVH:
        heads(0, 0)
    else:
        lax.fori_loop(0, KVH // head_block, heads, 0)
    if finishes:
        for k in range(KVH):
            pltpu.make_async_copy(held_ref.at[k], out_of(out_ref, k), sems.at[k]).wait()


def attend(form, numbers, queries, spans, state=()):
    row_count = queries.shape[0]
    groups = QH // KVH
    finishes = form in ("last", "only")
    arrays = [array for kind, listed in spans for array in listed]
    operands = [*numbers, queries, *arrays, *state]
    in_specs = [vmem if state else smem] * len(numbers) + [vmem] * (len(operands) - len(numbers))
    state_shape = [jax.ShapeDtypeStruct((KVH * row_count * groups, width), jnp.float32) for width in (2 * DH, DH)]
    scratch, aliases = [], {}
    if finishes:
        out_specs, out_shape = anywhere, jax.ShapeDtypeStruct(queries.shape, queries.dtype)
        scratch = [
            pltpu.VMEM((KVH, row_count, groups * DH), queries.dtype),
            pltpu.SemaphoreType.DMA((KVH,)),
        ]
    else:
        out_specs, out_shape = [vmem, vmem], state_shape
        if form == "first":
            out_specs.append(vmem)
            out_shape.append(jax.ShapeDtypeStruct((8, DH), jnp.int32))
        else:
            aliases = {len(operands) - 2: 0, len(operands) - 1: 1}
    key_count = sum(array.shape[0] for array in arrays)
    return pl.pallas_call(
        functools.partial(attend_kernel, tuple((kind, len(listed)) for kind, listed in spans), form),
        in_specs=in_specs,
        out_specs=out_specs,
        out_shape=out_shape,
        scratch_shapes=scratch,
        input_output_aliases=aliases,
        compiler_params=pltpu.CompilerParams(vmem_limit_bytes=kernel_vmem),
        cost_estimate=pl.CostEstimate(
            flops=4 * row_count * QH * DH * key_count,
            bytes_accessed=2 * row_count * QH * DH * 4,
            transcendentals=row_count * QH * key_count,
        ),
    )(*operands)


def stage_kernel(split, *refs):
    sems = refs[-1]
    copies, at = [], 0
    count = (len(refs) - 1 + split) // 3
    outs = refs[count:-1]
    for number, source in enumerate(refs[:count]):
        height = source.shape[0] if number < split else source.shape[0] // 2
        for start in range(0, source.shape[0], height):
            copies.append(pltpu.make_async_copy(source.at[start:start + height], outs[at], sems.at[at]))
            at += 1
    for copy in copies:
        copy.start()
    for copy in copies:
        copy.wait()


def stage(whole, halved):
    shapes = [jax.ShapeDtypeStruct(array.shape, array.dtype) for array in whole]
    for array in halved:
        shapes += [jax.ShapeDtypeStruct((array.shape[0] // 2, array.shape[1]), array.dtype)] * 2
    arrays = [pltpu.with_memory_space_constraint(array, pltpu.HBM) for array in (*whole, *halved)]
    return pl.pallas_call(
        functools.partial(stage_kernel, len(whole)),
        in_specs=[hbm] * len(arrays),
        out_specs=[vmem] * len(shapes),
        out_shape=shapes,
        scratch_shapes=[pltpu.SemaphoreType.DMA((len(shapes),))],
        compiler_params=pltpu.CompilerParams(vmem_limit_bytes=8 * 1024 * 1024),
    )(*arrays)


def pick_kernel(end_ref, middle_ref, out_ref):
    z = lax.axis_index("branch")
    at_end = (z == 0) | (z == lax.axis_size("branch") - 1)

    @pl.when(at_end)
    def _():
        out_ref[...] = end_ref[...]

    @pl.when(jnp.logical_not(at_end))
    def _():
        out_ref[...] = middle_ref[...]


def pick(end_rows, middle_rows):
    return pl.pallas_call(
        pick_kernel,
        in_specs=[vmem, vmem],
        out_specs=vmem,
        out_shape=jax.ShapeDtypeStruct(end_rows.shape, end_rows.dtype),
        compiler_params=pltpu.CompilerParams(vmem_limit_bytes=4 * 1024 * 1024),
    )(end_rows, middle_rows)


def gathered_body(queries, leaf_kv, branch_kv, root_kv, branch_len, leaf_len, leaf_parent):
    trunk_rows = lax.all_gather(branch_kv, "leaf", axis=0, tiled=True)
    whole_root = lax.all_gather(root_kv, ("branch", "leaf"), axis=0, tiled=True)
    numbers = (leaf_parent, branch_len, leaf_len)
    spans = [("leaf", [leaf_kv]), ("trunk", [trunk_rows]), ("root", [whole_root])]
    return attend("only", numbers, queries, spans)


def exchanged_body(queries, leaf_kv, branch_kv, root_kv, branch_len, leaf_len, leaf_parent):
    across = [(i, i ^ 2) for i in range(4)]
    beside = [(i, i ^ 1) for i in range(4)]
    near = [(i, i ^ 1) for i in range(4)]
    far = [(i, i ^ 3) for i in range(4)]
    cross = [(1, 0), (2, 3), (3, 1), (0, 2)]
    numbers = (leaf_parent, branch_len, leaf_len)

    def swap(rows):
        return lax.ppermute(rows, "leaf", beside)

    far_own = lax.ppermute(root_kv, "branch", far)
    near_own = lax.ppermute(root_kv, "branch", near)
    side = lax.ppermute(root_kv, "leaf", across)
    own_swapped = swap(root_kv)
    kept, own_leaf, own, low, high = stage((queries, leaf_kv, root_kv), (branch_kv,))
    low_side = lax.ppermute(low, "leaf", across)
    high_side = lax.ppermute(high, "leaf", across)
    low_swapped = swap(low)
    high_swapped = swap(high)
    *state, info = attend("first", numbers, kept, [("leaf", [own_leaf]), ("root", [own, own_swapped])])

    near_side = lax.ppermute(side, "branch", near)
    far_side = lax.ppermute(far_own, "leaf", across)
    cross_own = lax.ppermute(pick(own, far_own), "branch", cross)
    side_swapped = swap(side)
    near_own_swapped = swap(near_own)
    far_own_swapped = swap(far_own)
    low_side_swapped = swap(low_side)
    state = attend("middle", (), kept, [
        ("root", [side, near_own, far_own, side_swapped, near_own_swapped, far_own_swapped]),
    ], state)

    cross_side = lax.ppermute(pick(side, far_side), "branch", cross)
    near_side_swapped = swap(near_side)
    far_side_swapped = swap(far_side)
    state = attend("middle", (info,), kept, [
        (("held", 0), [low, low_side]),
        (("swapped", 0), [low_swapped, low_side_swapped]),
        ("root", [near_side, far_side, near_side_swapped, far_side_swapped]),
    ], state)

    cross_own_swapped = swap(cross_own)
    high_side_swapped = swap(high_side)
    cross_side_swapped = swap(cross_side)
    state = attend("middle", (info,), kept, [
        (("held", 1), [high, high_side]),
        (("swapped", 1), [high_swapped, high_side_swapped]),
        ("root", [cross_own, cross_own_swapped]),
    ], state)
    return attend("last", (info,), kept, [("root", [cross_side, cross_side_swapped])], state)


def solution(mesh):
    split = P(("rep", "branch", "leaf"), None)
    single = P(("rep", "branch", "leaf"))
    small = mesh.shape["branch"] == 4 and mesh.shape["leaf"] == 4
    return jax.shard_map(
        exchanged_body if small else gathered_body,
        mesh=mesh,
        in_specs=(split, split, split, split, P("rep"), single, single),
        out_specs=split,
        check_vma=False,
    )
```

```python
import functools
import math
import types

import jax
import jax.numpy as jnp
from jax import lax
from jax.experimental import pallas as pl
from jax.experimental.pallas import tpu as pltpu
from jax.sharding import PartitionSpec as P


QH = 32
KVH = 4
DH = 128
BR_DEV = 2
BL = 512


neg_large = -1e30
key_tile = 256
head_block = 4
group_block = 8
kernel_vmem = 28 * 1024 * 1024
vmem = pl.BlockSpec(memory_space=pltpu.VMEM)
smem = pl.BlockSpec(memory_space=pltpu.SMEM)
anywhere = pl.BlockSpec(memory_space=pl.ANY)
hbm = pl.BlockSpec(memory_space=pltpu.HBM)


def tiles_of(spans, scalars):
    tiles, pending, height = [], [], 0
    for kind, refs in spans:
        parts = []
        if kind == "leaf":
            tiles.append(([((refs[0], refs[0]), 0, refs[0].shape[0], None)], True))
        elif kind == "root":
            for ref in refs:
                for start in range(0, ref.shape[0], key_tile):
                    parts.append(((ref, ref), start, min(key_tile, ref.shape[0] - start), None))
        elif kind == "trunk":
            base = scalars.local_branch * BL
            for start in range(0, BL, key_tile):
                parts.append(((refs[0], refs[0]), base + start, key_tile, start))
        else:
            rows = refs[0].shape[0]
            place = scalars.core if kind[0] == "held" else 1 - scalars.core
            parts.append((tuple(refs), 0, rows, (place * 2 + kind[1]) * rows))
        for part in parts:
            pending.append(part)
            height += part[2]
            if height >= key_tile:
                tiles.append((pending, False))
                pending, height = [], 0
    if pending:
        tiles.append((pending, False))
    return tiles


def load(part, lanes, scalars):
    (near, far), start, size, token = part
    if not isinstance(start, int):
        start = pl.multiple_of(start, key_tile)
    rows = near[pl.ds(start, size), lanes]
    if far is not near:
        rows = jnp.where(
            scalars.elsewhere, far[pl.ds(start, size), lanes].astype(jnp.float32), rows.astype(jnp.float32)
        )
    return rows


def joined(parts):
    return parts[0] if len(parts) == 1 else jnp.concatenate(parts, axis=0)


def attend_kernel(kinds, form, *refs):
    refs = list(refs)
    reads_numbers, finishes = form in ("first", "only"), form in ("last", "only")
    masks = any(kind not in ("leaf", "root") for kind, count in kinds)
    if reads_numbers:
        parent_ref, length_ref, live_ref = [refs.pop(0) for _ in range(3)]
        parent = parent_ref[0]
        local_branch = parent - lax.axis_index("branch") * BR_DEV
        length, live_count = length_ref[parent], live_ref[0]
    elif masks or finishes:
        info = refs.pop(0)[...]
        elsewhere, length, live_count = info[0:1] > 0, info[1:2], info[2:3]
    query_ref = refs.pop(0)
    spans = [(kind, [refs.pop(0) for _ in range(count)]) for kind, count in kinds]
    carries = not reads_numbers
    if carries:
        old_total, old_max = refs.pop(0), refs.pop(0)
    if finishes:
        out_ref, held_ref, sems = refs
    else:
        total_ref, max_ref = refs.pop(0), refs.pop(0)
    place = lax.axis_index("leaf")
    if form == "first":
        info_ref = refs.pop(0)
        row = lax.broadcasted_iota(jnp.int32, info_ref.shape, 0)
        other = (local_branch != lax.div(place, 2)).astype(jnp.int32)
        info_ref[...] = jnp.where(row == 0, other, jnp.where(row == 1, length, live_count))
    scalars = types.SimpleNamespace()
    if masks:
        scalars.length, scalars.core = length, lax.rem(place, 2)
        if reads_numbers:
            scalars.local_branch = local_branch
        else:
            scalars.elsewhere = elsewhere
        seen_ref = [listed for kind, listed in spans if kind == "root"][0][0]
    tiles = tiles_of(spans, scalars)
    row_count = query_ref.shape[0]
    groups = query_ref.shape[1] // (DH * KVH)
    factor = DH ** -0.5 * math.log2(math.e)

    def lanes_at(number):
        start = number * DH
        return pl.ds(start if isinstance(start, int) else pl.multiple_of(start, DH), DH)

    def head(k, g0):
        total_rows = row_count * group_block
        start = (k * groups + g0) * row_count
        rows = pl.ds(start if isinstance(start, int) else pl.multiple_of(start, row_count), total_rows)
        query = jnp.concatenate(
            [query_ref[:, lanes_at(k * groups + g)] for g in range(g0, g0 + group_block)], axis=0
        )
        if carries:
            total = old_total[rows, :]
            row_max = old_max[rows, :]
        else:
            row_max, total = None, None
        for parts, causal in tiles:
            keys, values, ones = [], [], []
            for part in parts:
                key_rows = load(part, lanes_at(k), scalars)
                value_rows = load(part, lanes_at(KVH + k), scalars)
                one_rows = jnp.ones_like(value_rows)
                if part[3] is not None:
                    used = lax.broadcasted_iota(jnp.int32, key_rows.shape, 0) < scalars.length - part[3]
                    seen = seen_ref[:16, lanes_at(k)][:1].astype(jnp.float32)
                    key_rows = jnp.where(used, key_rows.astype(jnp.float32), seen).astype(query.dtype)
                    value_rows = jnp.where(used, value_rows.astype(jnp.float32), 0.0).astype(query.dtype)
                    one_rows = jnp.where(used, 1.0, 0.0).astype(query.dtype)
                keys.append(key_rows)
                values.append(value_rows)
                ones.append(one_rows)
            scores = lax.dot_general(
                query, joined(keys), (((1,), (1,)), ((), ())), preferred_element_type=jnp.float32
            )
            if causal:
                column = lax.broadcasted_iota(jnp.int32, scores.shape, 1)
                row = lax.rem(lax.broadcasted_iota(jnp.int32, scores.shape, 0), row_count)
                scores = jnp.where(column <= row, scores, neg_large)
            top = jnp.broadcast_to(jnp.max(scores, axis=1, keepdims=True), (total_rows, DH))
            new_max = top if row_max is None else jnp.maximum(row_max, top)
            wide = jnp.concatenate([new_max] * (scores.shape[1] // DH), axis=1)
            weights = jnp.exp2((scores - wide) * factor).astype(jnp.bfloat16)
            padded = jnp.concatenate([joined(values), joined(ones)], axis=1)
            product = jnp.dot(weights, padded, preferred_element_type=jnp.float32)
            if total is None:
                total = product
            else:
                shrink = jnp.exp2((row_max - new_max) * factor)
                total = total * jnp.concatenate([shrink, shrink], axis=1) + product
            row_max = new_max
        if finishes:
            result = total[:, :DH] * pl.reciprocal(total[:, DH:])
            live = lax.broadcasted_iota(jnp.int32, (row_count, DH), 0) < live_count
            for g in range(group_block):
                piece = result[g * row_count:(g + 1) * row_count]
                lanes = slice((g0 + g) * DH, (g0 + g + 1) * DH)
                held_ref[k, :, lanes] = jnp.where(live, piece, 0.0).astype(held_ref.dtype)
            if g0 + group_block == groups:
                pltpu.make_async_copy(held_ref.at[k], out_of(out_ref, k), sems.at[k]).start()
        else:
            total_ref[rows, :] = total
            max_ref[rows, :] = row_max

    def out_of(out_ref, k):
        width = groups * DH
        start = k * width
        return out_ref.at[:, pl.ds(start if isinstance(start, int) else pl.multiple_of(start, width), width)]

    def heads(step, unused):
        for extra in range(head_block):
            for g0 in range(0, groups, group_block):
                head(step * head_block + extra, g0)
        return unused

    if head_block == KVH:
        heads(0, 0)
    else:
        lax.fori_loop(0, KVH // head_block, heads, 0)
    if finishes:
        for k in range(KVH):
            pltpu.make_async_copy(held_ref.at[k], out_of(out_ref, k), sems.at[k]).wait()


def attend(form, numbers, queries, spans, state=()):
    row_count = queries.shape[0]
    groups = QH // KVH
    finishes = form in ("last", "only")
    arrays = [array for kind, listed in spans for array in listed]
    operands = [*numbers, queries, *arrays, *state]
    in_specs = [vmem if state else smem] * len(numbers) + [vmem] * (len(operands) - len(numbers))
    state_shape = [jax.ShapeDtypeStruct((KVH * row_count * groups, width), jnp.float32) for width in (2 * DH, DH)]
    scratch, aliases = [], {}
    if finishes:
        out_specs, out_shape = anywhere, jax.ShapeDtypeStruct(queries.shape, queries.dtype)
        scratch = [
            pltpu.VMEM((KVH, row_count, groups * DH), queries.dtype),
            pltpu.SemaphoreType.DMA((KVH,)),
        ]
    else:
        out_specs, out_shape = [vmem, vmem], state_shape
        if form == "first":
            out_specs.append(vmem)
            out_shape.append(jax.ShapeDtypeStruct((8, DH), jnp.int32))
        else:
            aliases = {len(operands) - 2: 0, len(operands) - 1: 1}
    key_count = sum(array.shape[0] for array in arrays)
    return pl.pallas_call(
        functools.partial(attend_kernel, tuple((kind, len(listed)) for kind, listed in spans), form),
        in_specs=in_specs,
        out_specs=out_specs,
        out_shape=out_shape,
        scratch_shapes=scratch,
        input_output_aliases=aliases,
        compiler_params=pltpu.CompilerParams(vmem_limit_bytes=kernel_vmem),
        cost_estimate=pl.CostEstimate(
            flops=4 * row_count * QH * DH * key_count,
            bytes_accessed=2 * row_count * QH * DH * 4,
            transcendentals=row_count * QH * key_count,
        ),
    )(*operands)


def stage_kernel(split, *refs):
    sems = refs[-1]
    copies, at = [], 0
    count = (len(refs) - 1 + split) // 3
    outs = refs[count:-1]
    for number, source in enumerate(refs[:count]):
        height = source.shape[0] if number < split else source.shape[0] // 2
        for start in range(0, source.shape[0], height):
            copies.append(pltpu.make_async_copy(source.at[start:start + height], outs[at], sems.at[at]))
            at += 1
    for copy in copies:
        copy.start()
    for copy in copies:
        copy.wait()


def stage(whole, halved):
    shapes = [jax.ShapeDtypeStruct(array.shape, array.dtype) for array in whole]
    for array in halved:
        shapes += [jax.ShapeDtypeStruct((array.shape[0] // 2, array.shape[1]), array.dtype)] * 2
    arrays = [pltpu.with_memory_space_constraint(array, pltpu.HBM) for array in (*whole, *halved)]
    return pl.pallas_call(
        functools.partial(stage_kernel, len(whole)),
        in_specs=[hbm] * len(arrays),
        out_specs=[vmem] * len(shapes),
        out_shape=shapes,
        scratch_shapes=[pltpu.SemaphoreType.DMA((len(shapes),))],
        compiler_params=pltpu.CompilerParams(vmem_limit_bytes=8 * 1024 * 1024),
    )(*arrays)


def pick_kernel(end_ref, middle_ref, out_ref):
    z = lax.axis_index("branch")
    at_end = (z == 0) | (z == lax.axis_size("branch") - 1)

    @pl.when(at_end)
    def _():
        out_ref[...] = end_ref[...]

    @pl.when(jnp.logical_not(at_end))
    def _():
        out_ref[...] = middle_ref[...]


def pick(end_rows, middle_rows):
    return pl.pallas_call(
        pick_kernel,
        in_specs=[vmem, vmem],
        out_specs=vmem,
        out_shape=jax.ShapeDtypeStruct(end_rows.shape, end_rows.dtype),
        compiler_params=pltpu.CompilerParams(vmem_limit_bytes=4 * 1024 * 1024),
    )(end_rows, middle_rows)


def gathered_body(queries, leaf_kv, branch_kv, root_kv, branch_len, leaf_len, leaf_parent):
    trunk_rows = lax.all_gather(branch_kv, "leaf", axis=0, tiled=True)
    whole_root = lax.all_gather(root_kv, ("branch", "leaf"), axis=0, tiled=True)
    numbers = (leaf_parent, branch_len, leaf_len)
    spans = [("leaf", [leaf_kv]), ("trunk", [trunk_rows]), ("root", [whole_root])]
    return attend("only", numbers, queries, spans)


def exchanged_body(queries, leaf_kv, branch_kv, root_kv, branch_len, leaf_len, leaf_parent):
    across = [(i, i ^ 2) for i in range(4)]
    beside = [(i, i ^ 1) for i in range(4)]
    near = [(i, i ^ 1) for i in range(4)]
    far = [(i, i ^ 3) for i in range(4)]
    cross = [(1, 0), (2, 3), (3, 1), (0, 2)]
    numbers = (leaf_parent, branch_len, leaf_len)

    def swap(rows):
        return lax.ppermute(rows, "leaf", beside)

    far_own = lax.ppermute(root_kv, "branch", far)
    near_own = lax.ppermute(root_kv, "branch", near)
    side = lax.ppermute(root_kv, "leaf", across)
    own_swapped = swap(root_kv)
    kept, own_leaf, own, low, high = stage((queries, leaf_kv, root_kv), (branch_kv,))
    low_side = lax.ppermute(low, "leaf", across)
    high_side = lax.ppermute(high, "leaf", across)
    low_swapped = swap(low)
    high_swapped = swap(high)
    *state, info = attend("first", numbers, kept, [("leaf", [own_leaf]), ("root", [own, own_swapped])])

    near_side = lax.ppermute(side, "branch", near)
    far_side = lax.ppermute(far_own, "leaf", across)
    cross_own = lax.ppermute(pick(own, far_own), "branch", cross)
    side_swapped = swap(side)
    near_own_swapped = swap(near_own)
    far_own_swapped = swap(far_own)
    low_side_swapped = swap(low_side)
    state = attend("middle", (), kept, [
        ("root", [side, near_own, far_own, side_swapped, near_own_swapped, far_own_swapped]),
    ], state)

    cross_side = lax.ppermute(pick(side, far_side), "branch", cross)
    near_side_swapped = swap(near_side)
    far_side_swapped = swap(far_side)
    state = attend("middle", (info,), kept, [
        ("root", [near_side, far_side, near_side_swapped, far_side_swapped]),
        (("held", 0), [low, low_side]),
        (("swapped", 0), [low_swapped, low_side_swapped]),
    ], state)

    cross_own_swapped = swap(cross_own)
    high_side_swapped = swap(high_side)
    cross_side_swapped = swap(cross_side)
    state = attend("middle", (info,), kept, [
        ("root", [cross_own, cross_own_swapped]),
        (("held", 1), [high, high_side]),
        (("swapped", 1), [high_swapped, high_side_swapped]),
    ], state)
    return attend("last", (info,), kept, [("root", [cross_side, cross_side_swapped])], state)


def solution(mesh):
    split = P(("rep", "branch", "leaf"), None)
    single = P(("rep", "branch", "leaf"))
    small = mesh.shape["branch"] == 4 and mesh.shape["leaf"] == 4
    return jax.shard_map(
        exchanged_body if small else gathered_body,
        mesh=mesh,
        in_specs=(split, split, split, split, P("rep"), single, single),
        out_specs=split,
        check_vma=False,
    )
```
